32 devices in a mesh: row: 8 (over z, x), col: 4 (over y, core).
Axes of the slice: x: 2, y: 2, z: 4, core: 2. Of those that a mesh axis runs over, the one named last changes fastest.
Arguments:
- tokens: bfloat16 [512, 8192], P('col', 'row'), may hold values from -6 to 6
- gate_weight: bfloat16 [8192, 14336], P('row', 'col'), may hold values from -0.09375 to 0.09375
- up_weight: bfloat16 [8192, 14336], P('row', 'col'), may hold values from -0.09375 to 0.09375
- down_weight: bfloat16 [14336, 8192], P('col', 'row'), may hold values from -0.09375 to 0.09375
- gate_mask: int32 [128, 224], P('row', 'col'), may hold values from 0 to 1, as said below
- up_mask: int32 [128, 224], P('row', 'col'), may hold values from 0 to 1, as said below
- down_mask: int32 [224, 128], P('col', 'row'), may hold values from 0 to 1, as said below
- head_weight: bfloat16 [8192, 128], P('row'), may hold values from -0.15625 to 0.15625
- labels: int32 [512], P('col'), may hold values from 0 to 127
Outputs:
- token_loss: float32 [512], P('col')
- tokens_grad: bfloat16 [512, 8192], P('col', 'row')
- gate_grad: bfloat16 [8192, 14336], P('row', 'col')
- up_grad: bfloat16 [8192, 14336], P('row', 'col')
- down_grad: bfloat16 [14336, 8192], P('col', 'row')
The draws below stay inside these ranges and needn't reach their ends.
Inputs may be any that keep to these rules, and one draw needn't show every extreme that they name: `gate_mask`: 1 keeps a block of 64 x 64 weights, 0 prunes it. `up_mask`: 1 keeps a block of 64 x 64 weights, 0 prunes it. `down_mask`: 1 keeps a block of 64 x 64 weights, 0 prunes it.
All inputs are finite; a program needn't handle non-finite values.
Results may differ from the reference program's by a relative error of at most 0.011.
Values may be sent and summed in bfloat16 or wider, within the bound.
A program may use at most 192 MiB of HBM per device.

```python
import jax
import jax.numpy as jnp
from jax import lax

D = 8192
FF = 14336
BLOCK = 64
CLASSES = 128
TOKENS = 512


def keep_blocks(key, height, breadth, by_rows):
    level_key, pick_key = jax.random.split(key)
    if by_rows:
        level = jax.random.randint(level_key, (height, 1), 1, 4)
    else:
        level = jax.random.randint(level_key, (1, breadth), 1, 4)
    picks = jax.random.randint(pick_key, (height, breadth), 0, 4)
    return (picks < level).astype(jnp.int32)


def draw_gate_mask(key, part):
    return keep_blocks(jax.random.fold_in(key, 11), D // BLOCK, FF // BLOCK, True)


def draw_up_mask(key, part):
    return keep_blocks(jax.random.fold_in(key, 23), D // BLOCK, FF // BLOCK, True)


def draw_down_mask(key, part):
    return keep_blocks(jax.random.fold_in(key, 37), FF // BLOCK, D // BLOCK, False)


def touch_ends(array, key, least, high):
    longest = array.shape.index(max(array.shape))
    spots = []
    for shift in (0, 1):
        where = [jax.random.randint(jax.random.fold_in(key, axis), (), 0, length) for axis, length in enumerate(array.shape)]
        where[longest] = (where[longest] + shift) % array.shape[longest]
        spots.append(tuple(where))
    return array.at[spots[0]].set(least).at[spots[1]].set(high)


def levels(own_key, shape, shards, low, largest):
    gain = 1.0
    for axis_at, parts in shards:
        steps = jax.random.uniform(jax.random.fold_in(jax.random.fold_in(own_key, 6), axis_at), (parts,), jnp.float32, low / len(shards), largest / len(shards))
        gain = gain * jnp.repeat(jnp.exp(steps), shape[axis_at] // parts).reshape((-1,) + (1,) * (len(shape) - 1 - axis_at))
    return gain


def noise(stream_key, dims, spread, reach, shards=(), held_as=jnp.bfloat16):
    gain = levels(stream_key, dims, shards, -0.22, 0.18) if shards else 1.0
    entries = jax.random.normal(stream_key, dims, jnp.float32) * spread * gain
    return jnp.minimum(jnp.maximum(entries, -reach), reach).astype(held_as)


def setup_inputs(seed: int = 0) -> dict:
    arg_keys = jax.random.split(jax.random.key(seed), 10)
    return {
        "tokens": noise(arg_keys[0], (TOKENS, D), 1.0, 6.0, ((0, 4), (1, 8))),
        "gate_weight": noise(arg_keys[1], (D, FF), (D // 2) ** -0.5, 0.09375, ((0, 8), (1, 4))),
        "up_weight": noise(arg_keys[2], (D, FF), (D // 2) ** -0.5, 0.09375, ((0, 8), (1, 4))),
        "down_weight": noise(arg_keys[3], (FF, D), (FF // 4) ** -0.5, 0.09375, ((0, 4), (1, 8))),
        "gate_mask": draw_gate_mask(jax.random.fold_in(arg_keys[9], 71), 0),
        "up_mask": draw_up_mask(jax.random.fold_in(arg_keys[9], 71), 0),
        "down_mask": draw_down_mask(jax.random.fold_in(arg_keys[9], 71), 0),
        "head_weight": noise(arg_keys[7], (D, CLASSES), (D // 6) ** -0.5, 0.15625, ((0, 8),)),
        "labels": touch_ends(jax.random.randint(arg_keys[8], (TOKENS,), 0, CLASSES), jax.random.fold_in(arg_keys[8], 1), 0, CLASSES - 1).astype(jnp.int32),
    }


loss_scale = 8.0


def masked(weight, block_mask):
    height, breadth = weight.shape
    blocks = weight.reshape(block_mask.shape[0], height // block_mask.shape[0], block_mask.shape[1], breadth // block_mask.shape[1])
    pruned = blocks * block_mask[:, None, :, None].astype(weight.dtype)
    return pruned.reshape(height, breadth)


def classify(logits, labels):
    exponent = jnp.exp(logits)
    partition = jnp.sum(exponent, axis=1, keepdims=True)
    classes = lax.broadcasted_iota(jnp.int32, logits.shape, 1)
    onehot = (labels[:, None] == classes).astype(jnp.float32)
    token_cost = jnp.log(partition[:, 0]) - jnp.sum(logits * onehot, axis=1)
    return token_cost, loss_scale * (exponent / partition - onehot)


def reference(tokens, gate_weight, up_weight, down_weight, gate_mask, up_mask, down_mask, head_weight, labels):
    gate_kept = masked(gate_weight, gate_mask)
    up_kept = masked(up_weight, up_mask)
    down_kept = masked(down_weight, down_mask)
    gate_sum = jnp.dot(tokens, gate_kept, preferred_element_type=jnp.float32)
    up_sum = jnp.dot(tokens, up_kept, preferred_element_type=jnp.float32)
    sigmoid_gate = jax.nn.sigmoid(gate_sum)
    activated = gate_sum * sigmoid_gate
    hidden = (activated * up_sum).astype(jnp.bfloat16)
    mixed_rows = (tokens.astype(jnp.float32) + jnp.dot(hidden, down_kept, preferred_element_type=jnp.float32)).astype(jnp.bfloat16)
    logits = jnp.dot(mixed_rows, head_weight, preferred_element_type=jnp.float32)
    token_loss, grad_full = classify(logits, labels)
    dlogits = grad_full.astype(jnp.bfloat16)
    dmixed = jnp.dot(dlogits, head_weight.T, preferred_element_type=jnp.float32).astype(jnp.bfloat16)
    dhidden = jnp.dot(dmixed, down_kept.T, preferred_element_type=jnp.float32)
    gate_delta = (dhidden * up_sum * sigmoid_gate * (1.0 + gate_sum * (1.0 - sigmoid_gate))).astype(jnp.bfloat16)
    up_delta = (dhidden * activated).astype(jnp.bfloat16)
    down_grad = masked(jnp.dot(hidden.T, dmixed, preferred_element_type=jnp.float32), down_mask).astype(jnp.bfloat16)
    gate_grad = masked(jnp.dot(tokens.T, gate_delta, preferred_element_type=jnp.float32), gate_mask).astype(jnp.bfloat16)
    up_grad = masked(jnp.dot(tokens.T, up_delta, preferred_element_type=jnp.float32), up_mask).astype(jnp.bfloat16)
    input_sum = jnp.dot(gate_delta, gate_kept.T, preferred_element_type=jnp.float32) + jnp.dot(up_delta, up_kept.T, preferred_element_type=jnp.float32)
    tokens_grad = (dmixed.astype(jnp.float32) + input_sum).astype(jnp.bfloat16)
    return (token_loss, tokens_grad, gate_grad, up_grad, down_grad)
```

```python
import functools

import jax
import jax.numpy as jnp
from jax import lax
from jax.experimental import pallas as pl
from jax.experimental.pallas import tpu as pltpu
from jax.sharding import PartitionSpec as P

loss_scale = 8.0
F32 = jnp.float32
BF16 = jnp.bfloat16
MESH = pl.DeviceIdType.MESH


def classify(logits, labels):
    exponent = jnp.exp(logits)
    partition = jnp.sum(exponent, axis=1, keepdims=True)
    classes = lax.broadcasted_iota(jnp.int32, logits.shape, 1)
    onehot = (labels[:, None] == classes).astype(F32)
    token_cost = jnp.log(partition[:, 0]) - jnp.sum(logits * onehot, axis=1)
    return (token_cost, loss_scale * (exponent / partition - onehot))


def tile_of(width):
    for tile in (512, 256, 128):
        if width % tile == 0:
            return tile
    return width


def widened(mask, width):
    return jnp.repeat(mask.astype(F32), width // mask.shape[1], axis=1)


def pruned(values, mask):
    height, breadth = values.shape
    blocks = mask.shape[0]
    split = values.reshape(blocks, height // blocks, breadth)
    kept = split * mask[:, None, :].astype(values.dtype)
    return kept.reshape(height, breadth)


def dot(a, b, a_axis, b_axis):
    return lax.dot_general(a, b, (((a_axis,), (b_axis,)), ((), ())), preferred_element_type=F32)


def run(body, grid, in_specs, out_specs, out_shape, flops, touched, scratch=()):
    return pl.pallas_call(
        body,
        grid=grid,
        in_specs=in_specs,
        out_specs=out_specs,
        out_shape=out_shape,
        scratch_shapes=list(scratch),
        compiler_params=pltpu.CompilerParams(vmem_limit_bytes=40 << 20),
        cost_estimate=pl.CostEstimate(flops=flops, bytes_accessed=touched, transcendentals=0),
    )


def gate_up_parts(x, gate, up, gate_mask, up_mask, rows):
    tokens, depth = x.shape
    width = gate.shape[1]
    tile = tile_of(width)
    blocks = gate_mask.shape[0]

    def body(x_ref, g_ref, u_ref, gm_ref, um_ref, o_ref):
        for k, (w, m) in enumerate(((g_ref, gm_ref), (u_ref, um_ref))):
            part = dot(x_ref[...], pruned(w[...], m[...]), 1, 0).astype(BF16)
            o_ref[:, k] = part.reshape(rows, tokens // rows, tile)

    weight = pl.BlockSpec((depth, tile), lambda j: (0, j))
    mask = pl.BlockSpec((blocks, tile), lambda j: (0, j))
    return run(
        body,
        (width // tile,),
        [pl.BlockSpec((tokens, depth), lambda j: (0, 0)), weight, weight, mask, mask],
        pl.BlockSpec((rows, 2, tokens // rows, tile), lambda j: (0, 0, 0, j)),
        jax.ShapeDtypeStruct((rows, 2, tokens // rows, width), BF16),
        4 * tokens * depth * width,
        4 * depth * width + 4 * tokens * width,
    )(x, gate, up, gate_mask, up_mask)


def down_part(hidden, down, mask):
    tokens, width = hidden.shape
    depth = down.shape[1]
    tile = tile_of(width)
    steps = width // tile
    mask = mask.reshape(steps, -1, depth)

    def body(h_ref, w_ref, m_ref, o_ref, acc):
        j = pl.program_id(0)
        part = dot(h_ref[...], pruned(w_ref[...], m_ref[0]), 1, 0)

        @pl.when(j == 0)
        def _():
            acc[...] = part

        @pl.when(j > 0)
        def _():
            acc[...] += part

        @pl.when(j == steps - 1)
        def _():
            o_ref[...] = acc[...].astype(BF16)

    return run(
        body,
        (steps,),
        [
            pl.BlockSpec((tokens, tile), lambda j: (0, j)),
            pl.BlockSpec((tile, depth), lambda j: (j, 0)),
            pl.BlockSpec((1, mask.shape[1], depth), lambda j: (j, 0, 0)),
        ],
        pl.BlockSpec((tokens, depth), lambda j: (0, 0)),
        jax.ShapeDtypeStruct((tokens, depth), BF16),
        2 * tokens * depth * width,
        2 * depth * width + 2 * tokens * width,
        [pltpu.VMEM((tokens, depth), F32)],
    )(hidden, down, mask)


def dhidden_part(dmixed, down, mask):
    tokens, depth = dmixed.shape
    width = down.shape[0]
    tile = tile_of(width)
    steps = width // tile
    mask = mask.reshape(steps, -1, depth)

    def body(d_ref, w_ref, m_ref, o_ref):
        o_ref[...] = dot(d_ref[...], pruned(w_ref[...], m_ref[0]), 1, 1).astype(BF16)

    return run(
        body,
        (steps,),
        [
            pl.BlockSpec((tokens, depth), lambda j: (0, 0)),
            pl.BlockSpec((tile, depth), lambda j: (j, 0)),
            pl.BlockSpec((1, mask.shape[1], depth), lambda j: (j, 0, 0)),
        ],
        pl.BlockSpec((tokens, tile), lambda j: (0, j)),
        jax.ShapeDtypeStruct((tokens, width), BF16),
        2 * tokens * depth * width,
        2 * depth * width + 2 * tokens * width,
    )(dmixed, down, mask)


def input_part(gate_delta, up_delta, gate, up, gate_mask, up_mask):
    tokens, width = gate_delta.shape
    depth = gate.shape[0]
    tile = tile_of(width)
    steps = width // tile
    blocks = gate_mask.shape[0]

    def body(gd_ref, ud_ref, g_ref, u_ref, gm_ref, um_ref, o_ref, acc):
        j = pl.program_id(0)
        part = dot(gd_ref[...], pruned(g_ref[...], gm_ref[...]), 1, 1)
        part += dot(ud_ref[...], pruned(u_ref[...], um_ref[...]), 1, 1)

        @pl.when(j == 0)
        def _():
            acc[...] = part

        @pl.when(j > 0)
        def _():
            acc[...] += part

        @pl.when(j == steps - 1)
        def _():
            o_ref[...] = acc[...].astype(BF16)

    delta = pl.BlockSpec((tokens, tile), lambda j: (0, j))
    weight = pl.BlockSpec((depth, tile), lambda j: (0, j))
    mask = pl.BlockSpec((blocks, tile), lambda j: (0, j))
    return run(
        body,
        (steps,),
        [delta, delta, weight, weight, mask, mask],
        pl.BlockSpec((tokens, depth), lambda j: (0, 0)),
        jax.ShapeDtypeStruct((tokens, depth), BF16),
        4 * tokens * depth * width,
        4 * depth * width + 4 * tokens * width,
        [pltpu.VMEM((tokens, depth), F32)],
    )(gate_delta, up_delta, gate, up, gate_mask, up_mask)


def column_grad(x, delta, mask):
    tokens, depth = x.shape
    width = delta.shape[1]
    tile = tile_of(width)
    blocks = mask.shape[0]

    def body(x_ref, d_ref, m_ref, o_ref):
        o_ref[...] = pruned(dot(x_ref[...], d_ref[...], 0, 0), m_ref[...]).astype(BF16)

    return run(
        body,
        (width // tile,),
        [
            pl.BlockSpec((tokens, depth), lambda j: (0, 0)),
            pl.BlockSpec((tokens, tile), lambda j: (0, j)),
            pl.BlockSpec((blocks, tile), lambda j: (0, j)),
        ],
        pl.BlockSpec((depth, tile), lambda j: (0, j)),
        jax.ShapeDtypeStruct((depth, width), BF16),
        2 * tokens * depth * width,
        2 * depth * width + 2 * tokens * width,
    )(x, delta, mask)


def row_grad(hidden, dmixed, mask):
    tokens, width = hidden.shape
    depth = dmixed.shape[1]
    tile = tile_of(width)
    steps = width // tile
    mask = mask.reshape(steps, -1, depth)

    def body(h_ref, d_ref, m_ref, o_ref):
        o_ref[...] = pruned(dot(h_ref[...], d_ref[...], 0, 0), m_ref[0]).astype(BF16)

    return run(
        body,
        (steps,),
        [
            pl.BlockSpec((tokens, tile), lambda j: (0, j)),
            pl.BlockSpec((tokens, depth), lambda j: (0, 0)),
            pl.BlockSpec((1, mask.shape[1], depth), lambda j: (j, 0, 0)),
        ],
        pl.BlockSpec((tile, depth), lambda j: (j, 0)),
        jax.ShapeDtypeStruct((width, depth), BF16),
        2 * tokens * depth * width,
        2 * depth * width + 2 * tokens * width,
    )(hidden, dmixed, mask)


def grid_of(axis, fast, size):
    me = lax.axis_index(axis)
    return me, lax.div(me, fast), lax.rem(me, fast), size // fast


def greet(axis, slow, quick, slows, fast):
    barrier = pltpu.get_barrier_semaphore()
    for d in range(1, fast):
        there = slow * fast + lax.rem(quick + d, fast)
        pl.semaphore_signal(barrier, inc=1, device_id={axis: there}, device_id_type=MESH)
    for d in range(1, slows):
        there = lax.rem(slow + d, slows) * fast + quick
        pl.semaphore_signal(barrier, inc=1, device_id={axis: there}, device_id_type=MESH)
    pl.semaphore_wait(barrier, fast + slows - 2)


def send(src, dst, sems, where, axis, there):
    copy = pltpu.make_async_remote_copy(
        src_ref=src,
        dst_ref=dst,
        send_sem=sems[0].at[where],
        recv_sem=sems[1].at[where],
        device_id={axis: there},
        device_id_type=MESH,
    )
    copy.start()
    return copy


def talking(call_id):
    return pltpu.CompilerParams(
        collective_id=call_id, has_side_effects=True, vmem_limit_bytes=56 << 20
    )


def both(*dims):
    return [pltpu.SemaphoreType.DMA(dims), pltpu.SemaphoreType.DMA(dims)]


def reduce_scatter(parts, axis, fast, slices, call_id):
    size, height, width = parts.shape
    slows = size // fast
    step = height // slices
    group = 16

    def body(p_ref, o_ref, xbuf, ybuf, zbuf, *sems):
        xsems, zsems = sems[:2], sems[2:]
        _, slow, quick, _ = grid_of(axis, fast, size)
        greet(axis, slow, quick, slows, fast)
        order = [(d, s) for s in range(slices) for d in [*range(1, slows), 0]]
        xcopies, zcopies = {}, {}
        for d, s in order:
            a = lax.rem(slow + d, slows)
            cut = pl.ds(s * step, step)
            for e in range(1, fast):
                b = lax.rem(quick + e, fast)
                xcopies[d, s, e] = send(
                    p_ref.at[a * fast + b, cut],
                    xbuf.at[e - 1, d, cut],
                    xsems,
                    (d * slices + s) * (fast - 1) + e - 1,
                    axis,
                    slow * fast + b,
                )
        for d, s in order:
            a = lax.rem(slow + d, slows)
            for e in range(1, fast):
                xcopies[d, s, e].wait_recv()

            def add(i, carry, d=d, s=s, a=a):
                at = pl.ds(pl.multiple_of(s * step + i * group, group), group)
                total = p_ref[a * fast + quick, at].astype(F32)
                for e in range(1, fast):
                    total += xbuf[e - 1, d, at].astype(F32)
                if d == 0:
                    o_ref[at] = total
                else:
                    ybuf[d - 1, at] = total.astype(BF16)
                return carry

            lax.fori_loop(0, step // group, add, 0)
            if d:
                cut = pl.ds(s * step, step)
                zcopies[d, s] = send(
                    ybuf.at[d - 1, cut],
                    zbuf.at[d - 1, cut],
                    zsems,
                    (d - 1) * slices + s,
                    axis,
                    a * fast + quick,
                )
        for s in range(slices):
            for d in range(1, slows):
                zcopies[d, s].wait_recv()

            def close(i, carry, s=s):
                at = pl.ds(pl.multiple_of(s * step + i * group, group), group)
                total = o_ref[at]
                for d in range(1, slows):
                    total += zbuf[d - 1, at].astype(F32)
                o_ref[at] = total
                return carry

            lax.fori_loop(0, step // group, close, 0)
        for copy in [*xcopies.values(), *zcopies.values()]:
            copy.wait_send()

    return pl.pallas_call(
        body,
        in_specs=[pl.BlockSpec(memory_space=pltpu.VMEM)],
        out_specs=pl.BlockSpec(memory_space=pltpu.VMEM),
        out_shape=jax.ShapeDtypeStruct((height, width), F32),
        scratch_shapes=[
            pltpu.VMEM((fast - 1, slows, height, width), BF16),
            pltpu.VMEM((slows - 1, height, width), BF16),
            pltpu.VMEM((slows - 1, height, width), BF16),
            *both(slows * slices * (fast - 1)),
            *both((slows - 1) * slices),
        ],
        compiler_params=talking(call_id),
    )(parts)


def gather(blocks, axis, size, fast, slices, call_id):
    height, width = blocks[0].shape
    slows = size // fast
    step = height // slices
    count = len(blocks)

    def body(*refs):
        ins, outs = refs[:count], refs[count : 2 * count]
        local, *sems = refs[2 * count :]
        xsems, zsems = sems[:2], sems[2:]
        me, slow, quick, _ = grid_of(axis, fast, size)
        greet(axis, slow, quick, slows, fast)
        order = [(k, s) for k in range(count) for s in range(slices)]
        copies, zcopies = [], {}

        def across(k, s, d, src, slot):
            cut = pl.ds(s * step, step)
            for e in range(1, fast):
                b = lax.rem(quick + e, fast)
                where = ((k * slices + s) * slows + d) * (fast - 1) + e - 1
                copies.append(
                    send(src, outs[k].at[slot, cut], xsems, where, axis, slow * fast + b)
                )

        keep = []
        for k, s in order:
            cut = pl.ds(s * step, step)
            for d in range(1, slows):
                there = lax.rem(slow + d, slows) * fast + quick
                zcopies[k, s, d] = send(
                    ins[k].at[cut],
                    outs[k].at[me, cut],
                    zsems,
                    (k * slices + s) * (slows - 1) + d - 1,
                    axis,
                    there,
                )
            across(k, s, 0, ins[k].at[cut], me)
        for k in range(count):
            keep.append(pltpu.make_async_copy(ins[k], outs[k].at[me], local.at[k]))
            keep[-1].start()
        for k, s in order:
            cut = pl.ds(s * step, step)
            for d in range(1, slows):
                slot = lax.rem(slow + slows - d, slows) * fast + quick
                zcopies[k, s, d].wait_recv()
                across(k, s, d, outs[k].at[slot, cut], slot)
        for copy in copies:
            copy.wait()
        for copy in zcopies.values():
            copy.wait_send()
        for copy in keep:
            copy.wait()

    got = pl.pallas_call(
        body,
        in_specs=[pl.BlockSpec(memory_space=pltpu.VMEM)] * count,
        out_specs=[pl.BlockSpec(memory_space=pl.ANY)] * count,
        out_shape=[jax.ShapeDtypeStruct((size, height, width), BF16)] * count,
        scratch_shapes=[
            pltpu.SemaphoreType.DMA((count,)),
            *both(count * slices * slows * (fast - 1)),
            *both(count * slices * (slows - 1)),
        ],
        compiler_params=talking(call_id),
    )(*blocks)
    return [whole.reshape(size * height, width) for whole in got]


def total_over(part, axis, size, fast, call_id):
    height, width = part.shape
    slows = size // fast

    def body(p_ref, o_ref, xbuf, ysum, zbuf, *sems):
        xsems, zsems = sems[:2], sems[2:]
        _, slow, quick, _ = grid_of(axis, fast, size)
        greet(axis, slow, quick, slows, fast)
        copies = []
        for e in range(1, fast):
            b = lax.rem(quick + e, fast)
            copies.append(send(p_ref, xbuf.at[quick], xsems, e - 1, axis, slow * fast + b))
        xbuf[quick] = p_ref[...]
        for copy in copies:
            copy.wait()
        total = xbuf[0]
        for b in range(1, fast):
            total += xbuf[b]
        ysum[...] = total
        copies = []
        for d in range(1, slows):
            there = lax.rem(slow + d, slows) * fast + quick
            copies.append(send(ysum, zbuf.at[slow], zsems, d - 1, axis, there))
        zbuf[slow] = total
        for copy in copies:
            copy.wait()
        total = zbuf[0]
        for a in range(1, slows):
            total += zbuf[a]
        o_ref[...] = total

    return pl.pallas_call(
        body,
        in_specs=[pl.BlockSpec(memory_space=pltpu.VMEM)],
        out_specs=pl.BlockSpec(memory_space=pltpu.VMEM),
        out_shape=jax.ShapeDtypeStruct((height, width), F32),
        scratch_shapes=[
            pltpu.VMEM((fast, height, width), F32),
            pltpu.VMEM((height, width), F32),
            pltpu.VMEM((slows, height, width), F32),
            *both(fast - 1),
            *both(slows - 1),
        ],
        compiler_params=talking(call_id),
    )(part)


def shards(
    rows, cols, tokens, gate_weight, up_weight, down_weight, gate_mask, up_mask, down_mask, head_weight, labels
):
    width = gate_weight.shape[1]
    gate_mask = widened(gate_mask, width)
    up_mask = widened(up_mask, width)
    down_mask = widened(down_mask, down_weight.shape[1])
    near = rows // 4
    mine = tokens.shape[0]
    (every_token,) = gather([tokens], "col", cols, 2, 2, 1)
    parts = gate_up_parts(every_token, gate_weight, up_weight, gate_mask, up_mask, rows)
    share = parts.shape[2]
    stacked = reduce_scatter(parts.reshape(rows, 2 * share, width), "row", near, 4, 2)
    gate_sum, up_sum = stacked[:share], stacked[share:]
    sigmoid_gate = jax.nn.sigmoid(gate_sum)
    activated = gate_sum * sigmoid_gate
    hidden = (activated * up_sum).astype(BF16)
    (hidden_all,) = gather([hidden], "row", rows, near, 4, 3)
    branch = reduce_scatter(
        down_part(hidden_all, down_weight, down_mask).reshape(cols, mine, -1), "col", 2, 2, 4
    )
    mixed_rows = (tokens.astype(F32) + branch).astype(BF16)
    partial_value = jnp.dot(mixed_rows, head_weight, preferred_element_type=F32)
    logits = total_over(partial_value, "row", rows, near, 5)
    token_loss, grad_full = classify(logits, labels)
    dlogits = grad_full.astype(BF16)
    dmixed = dot(dlogits, head_weight, 1, 1).astype(BF16)
    (dmixed_all,) = gather([dmixed], "col", cols, 2, 2, 6)
    dhidden = reduce_scatter(
        dhidden_part(dmixed_all, down_weight, down_mask).reshape(rows, share, width), "row", near, 4, 7
    )
    gate_delta = (dhidden * up_sum * sigmoid_gate * (1.0 + gate_sum * (1.0 - sigmoid_gate))).astype(BF16)
    up_delta = (dhidden * activated).astype(BF16)
    gate_all, up_all = gather([gate_delta, up_delta], "row", rows, near, 4, 8)
    down_grad = row_grad(hidden_all, dmixed_all, down_mask)
    gate_grad = column_grad(every_token, gate_all, gate_mask)
    up_grad = column_grad(every_token, up_all, up_mask)
    input_sum = lax.psum_scatter(
        input_part(gate_all, up_all, gate_weight, up_weight, gate_mask, up_mask),
        "col",
        scatter_dimension=0,
        tiled=True,
    ).astype(F32)
    tokens_grad = (dmixed.astype(F32) + input_sum).astype(BF16)
    return (token_loss, tokens_grad, gate_grad, up_grad, down_grad)


def solution(mesh):
    placed = (
        P("col", "row"),
        P("row", "col"),
        P("row", "col"),
        P("col", "row"),
        P("row", "col"),
        P("row", "col"),
        P("col", "row"),
        P("row", None),
        P("col"),
    )
    return jax.shard_map(
        functools.partial(shards, mesh.shape["row"], mesh.shape["col"]),
        mesh=mesh,
        in_specs=placed,
        out_specs=(P("col"), P("col", "row"), P("row", "col"), P("row", "col"), P("col", "row")),
        check_vma=False,
    )
```
